32 devices in a mesh: row: 16 (over z, x, core), col: 2 (over y).
Axes of the slice: x: 2, y: 2, z: 4, core: 2. Of those that a mesh axis runs over, the one named last changes fastest.
Arguments:
- token_ids: int32 [512], P('col'), may hold values from 0 to 50559, as said below
- table: bfloat16 [50560, 5120], P('row', 'col'), may hold values from -120 to 120
- norm_gain: float32 [5120], replicated, may hold values from 0.5 to 1.5
- w_qkv: bfloat16 [5120, 7168], P('col', 'row'), may hold values from -0.078125 to 0.078125
- w_gate: bfloat16 [5120, 16384], P('col', 'row'), may hold values from -0.078125 to 0.078125
- w_up: bfloat16 [5120, 16384], P('col', 'row'), may hold values from -0.078125 to 0.078125
Outputs:
- qkv_out: bfloat16 [512, 7168], P('col', 'row')
- hidden: bfloat16 [512, 16384], P('col', 'row')
The draws below stay inside these ranges and needn't reach their ends.
Inputs may be any that keep to these rules, and one draw needn't show every extreme that they name: `token_ids`: most ids of the micro-batch lie in one block of 3160 entries that starts at a multiple of 3160, which block being drawn; the others lie in the other blocks.
All inputs are finite; a program needn't handle non-finite values.
Results may differ from the reference program's by a relative error of at most 0.0058.
Values may be sent and summed in bfloat16 or wider, within the bound.
A program may use at most 128 MiB of HBM per device.

```python
import jax
import jax.numpy as jnp
from jax import lax

D = 5120
FF = 16384
VOC_DEV = 3160
QKV = 7168
VOCAB = 50560
TOKENS = 512


def draw_token_ids(key, part):
    main_key, away_key, inner_key, other_key = jax.random.split(jax.random.fold_in(key, 7), 4)
    shard_count = VOCAB // VOC_DEV
    main_shard = jax.random.randint(main_key, (), 0, shard_count)
    inner_ids = jax.random.randint(inner_key, (TOKENS,), 0, VOC_DEV)
    positions = jnp.arange(TOKENS, dtype=jnp.int32)
    away_mask = (jax.random.randint(away_key, (TOKENS,), 0, 16) == 0) | (positions == TOKENS - 1)
    other_shard = (main_shard + 1 + jax.random.randint(other_key, (TOKENS,), 0, shard_count - 1)) % shard_count
    chosen = jnp.where(away_mask, other_shard, main_shard)
    return (chosen * VOC_DEV + inner_ids).astype(jnp.int32)


def draw_table(key, part):
    noise_key, row_key, col_key = jax.random.split(key, 3)
    row_power = jax.random.uniform(row_key, (VOCAB, 1), jnp.float32)
    col_place = jnp.arange(D, dtype=jnp.float32)[None, :] / (D - 1)
    col_power = 0.5 * col_place + 0.5 * jax.random.uniform(col_key, (1, D), jnp.float32)
    scales = 0.3 * jnp.power(10.0, row_power + col_power)
    basis = jnp.clip(jax.random.normal(noise_key, (VOCAB, D), jnp.float32), -4.0, 4.0)
    return (basis * scales).astype(jnp.bfloat16)


def level_of(own_key, shape, shards, least, top_value):
    factor_of, own = 1.0, jax.random.fold_in(own_key, 6)
    for axis_at, shards_of in shards:
        heights = jnp.exp(jax.random.uniform(jax.random.fold_in(own, axis_at), (shards_of,), jnp.float32, least / len(shards), top_value / len(shards)))
        factor_of = factor_of * jnp.repeat(heights, shape[axis_at] // shards_of).reshape([-1 if axis == axis_at else 1 for axis in range(len(shape))])
    return factor_of


def gaussian(stream_key, dims, scale, most, cuts=(), held_as=jnp.bfloat16):
    gain = level_of(stream_key, dims, cuts, -0.22, 0.18) if cuts else 1.0
    values = jax.random.normal(stream_key, dims, jnp.float32) * scale * gain
    return jnp.minimum(jnp.maximum(values, -most), most).astype(held_as)


def setup_inputs(seed: int = 0) -> dict:
    seeds = jax.random.split(jax.random.key(seed), 7)
    return {
        "token_ids": draw_token_ids(jax.random.fold_in(seeds[6], 71), 0),
        "table": draw_table(jax.random.fold_in(seeds[6], 71), 0),
        "norm_gain": jnp.clip(1.0 + 0.1 * jax.random.normal(seeds[2], (D,), jnp.float32), 0.5, 1.5),
        "w_qkv": gaussian(seeds[3], (D, QKV), D ** -0.5, 0.078125, ((0, 2), (1, 16))),
        "w_gate": gaussian(seeds[4], (D, FF), D ** -0.5, 0.078125, ((0, 2), (1, 16))),
        "w_up": gaussian(seeds[5], (D, FF), D ** -0.5, 0.078125, ((0, 2), (1, 16))),
    }


def reference(token_ids, table, norm_gain, w_qkv, w_gate, w_up):
    embedded = jnp.take(table, token_ids.astype(jnp.int32), axis=0)
    values = embedded.astype(jnp.float32)
    factor = lax.rsqrt(lax.optimization_barrier(jnp.mean(values * values, axis=1, keepdims=True)) + 1e-05)
    normed = (values * factor * norm_gain[None, :].astype(jnp.float32)).astype(jnp.bfloat16)
    qkv_out = jnp.dot(normed, w_qkv, preferred_element_type=jnp.float32).astype(jnp.bfloat16)
    gate_values = jnp.dot(normed, w_gate, preferred_element_type=jnp.float32)
    up_values = jnp.dot(normed, w_up, preferred_element_type=jnp.float32)
    hidden = (jax.nn.silu(gate_values) * up_values).astype(jnp.bfloat16)
    return (qkv_out, hidden)
```

```python
import functools

import jax
import jax.numpy as jnp
from jax import lax
from jax.experimental import pallas as pl
from jax.experimental.pallas import tpu as pltpu
from jax.sharding import PartitionSpec as P

eps = 1e-05
CHUNKS = 4


def kernel(
    n_row, n_col, chunks, width, features,
    part_ref, gain_ref, wq_hbm, wg_hbm, wu_hbm,
    q_ref, h_ref,
    wq, wg, wu, crs, xsend, xrs, zown, zin, zfar_out, znear_out, act, xbuf, pf, ysend, yrecv,
    w_sem, core_s, core_r, x_s, x_r, zf_s, zn_s, z_r, xa_s, xa_r, ca_s, ca_r, y_s, y_r,
):
    row = lax.axis_index("row")
    col = lax.axis_index("col")
    k = row % 2
    xx = (row // 2) % 2
    z = row // 4
    nz = n_row // 4
    upper = z // (nz // 2)
    sgn = 1 - 2 * upper
    core_peer = row + 1 - 2 * k
    x_peer = row + 2 - 4 * xx
    far_peer = row + 4 * sgn
    near_peer = row - 4 * sgn
    inner = jnp.logical_and(z > 0, z < nz - 1)
    q_own = 2 * k + xx
    q_x = 2 * k + 1 - xx
    q_c0 = 2 * (1 - k) + xx
    q_c1 = 2 * (1 - k) + 1 - xx
    near_slot, far_slot = upper, 1 - upper
    dk = part_ref.shape[3]
    t4 = part_ref.shape[2]
    nq, nf = wq.shape[1], wg.shape[1]
    qo = 2 * nf

    w_copies = [
        pltpu.make_async_copy(wg_hbm, wg, w_sem.at[0]),
        pltpu.make_async_copy(wu_hbm, wu, w_sem.at[1]),
        pltpu.make_async_copy(wq_hbm, wq, w_sem.at[2]),
    ]
    for copy in w_copies:
        copy.start()

    barrier = pltpu.get_barrier_semaphore()

    def greet(where):
        pl.semaphore_signal(barrier, inc=1, device_id=where, device_id_type=pl.DeviceIdType.MESH)

    greet({"row": core_peer})
    greet({"row": x_peer})
    greet({"row": far_peer})
    for d in range(1, n_col):
        greet({"col": (col + d) % n_col})

    @pl.when(inner)
    def _():
        greet({"row": near_peer})

    @pl.when(inner)
    def _():
        pl.semaphore_wait(barrier, 4 + n_col - 1)

    @pl.when(jnp.logical_not(inner))
    def _():
        pl.semaphore_wait(barrier, 3 + n_col - 1)

    def rcopy(src, dst, s, r, where):
        return pltpu.make_async_remote_copy(
            src_ref=src, dst_ref=dst, send_sem=s, recv_sem=r,
            device_id=where, device_id_type=pl.DeviceIdType.MESH,
        )

    def core_rs(c):
        return rcopy(part_ref.at[c, pl.ds(2 * (1 - k), 2)], crs.at[c], core_s.at[c], core_r.at[c], {"row": core_peer})

    def x_rs(c):
        return rcopy(xsend.at[c], xrs.at[c], x_s.at[c], x_r.at[c], {"row": x_peer})

    def z_far_end(c):
        return rcopy(zown.at[c], zin.at[upper, c], zf_s.at[c], z_r.at[upper, c], {"row": far_peer})

    def z_far_inner(c):
        return rcopy(zfar_out.at[c], zin.at[upper, c], zf_s.at[c], z_r.at[upper, c], {"row": far_peer})

    def z_near(c):
        return rcopy(znear_out.at[c], zin.at[1 - upper, c], zn_s.at[c], z_r.at[1 - upper, c], {"row": near_peer})

    def z_wait(slot, c):
        rcopy(zown.at[c], zin.at[slot, c], zf_s.at[c], z_r.at[slot, c], {"row": far_peer}).wait_recv()

    def x_ag(c, q):
        return rcopy(act.at[c, q], act.at[c, q], xa_s.at[c], xa_r.at[c], {"row": x_peer})

    def core_ag(c, q, i):
        return rcopy(act.at[c, q], act.at[c, q], ca_s.at[c, i], ca_r.at[c, i], {"row": core_peer})

    def y_send(c, d):
        peer = (col + d) % n_col
        return rcopy(ysend.at[c, peer], yrecv.at[c, col], y_s.at[c, d - 1], y_r.at[c, col], {"col": peer})

    def y_wait(c, d):
        peer = (col + d) % n_col
        rcopy(ysend.at[c, peer], yrecv.at[c, peer], y_s.at[c, d - 1], y_r.at[c, peer], {"col": peer}).wait_recv()

    def at_stage(t, s, run):
        c = t - s

        @pl.when(jnp.logical_and(c >= 0, c < chunks))
        def _():
            run(c)

    def s0(c):
        core_rs(c).start()

    def s1(c):
        core_rs(c).wait_recv()
        xsend[c] = part_ref[c, q_x] + crs[c, 1 - xx]
        x_rs(c).start()
        zown[c] = part_ref[c, q_own] + crs[c, xx]

    def s2(c):
        x_rs(c).wait_recv()
        zown[c] = zown[c] + xrs[c]

        @pl.when(jnp.logical_not(inner))
        def _():
            z_far_end(c).start()

    def s3(c):
        @pl.when(inner)
        def _():
            z_wait(near_slot, c)
            zfar_out[c] = zown[c] + zin[near_slot, c]
            z_far_inner(c).start()

    def s4(c):
        z_wait(far_slot, c)

        @pl.when(inner)
        def _():
            znear_out[c] = zown[c] + zin[far_slot, c]
            z_near(c).start()
            act[c, q_own] = zfar_out[c] + zin[far_slot, c]

        @pl.when(jnp.logical_not(inner))
        def _():
            act[c, q_own] = zown[c] + zin[far_slot, c]

        x_ag(c, q_own).start()
        core_ag(c, q_own, 0).start()

    def s5(c):
        x_ag(c, q_x).wait_recv()
        core_ag(c, q_x, 1).start()

    def s6(c):
        core_ag(c, q_c0, 0).wait_recv()
        core_ag(c, q_c1, 1).wait_recv()

        @pl.when(c == 0)
        def _():
            for copy in w_copies:
                copy.wait()

        gain = gain_ref[:, pl.ds(pl.multiple_of(col * dk, 128), dk)]
        toks = 4 * t4
        values = act[c].reshape(toks, dk).astype(jnp.float32)
        squares = jnp.sum(values * values, axis=1, keepdims=True)
        xbuf[...] = (values * gain).astype(jnp.bfloat16)
        high = squares.astype(jnp.bfloat16)
        low = (squares - high.astype(jnp.float32)).astype(jnp.bfloat16)
        rows = toks // n_col
        tail = width - qo - nq
        lane = lax.broadcasted_iota(jnp.int32, (toks, tail), 1)
        pf[c, :, :, qo + nq:] = jnp.broadcast_to(squares, (toks, tail)).reshape(n_col, rows, tail)
        both = jnp.where(lane == 0, high.astype(jnp.float32), low.astype(jnp.float32)).astype(jnp.bfloat16)
        ysend[c, :, :, qo + nq:] = both.reshape(n_col, rows, tail)
        tile = 256

        def put(start, out, size):
            out = out.reshape(n_col, rows, size)
            pf[c, :, :, pl.ds(start, size)] = out
            ysend[c, :, :, pl.ds(start, size)] = out.astype(jnp.bfloat16)

        def tiles(j, carry):
            at = pl.multiple_of(j * tile, tile)
            put(at, jnp.dot(xbuf[...], wg[:, pl.ds(at, tile)], preferred_element_type=jnp.float32), tile)
            put(
                pl.multiple_of(nf + j * tile, tile),
                jnp.dot(xbuf[...], wu[:, pl.ds(at, tile)], preferred_element_type=jnp.float32), tile,
            )
            return carry

        lax.fori_loop(0, nf // tile, tiles, 0)
        put(qo, jnp.dot(xbuf[...], wq[...], preferred_element_type=jnp.float32), nq)
        for d in range(1, n_col):
            y_send(c, d).start()

    def s7(c):
        for d in range(1, n_col):
            y_wait(c, d)
        peers = [(col + d) % n_col for d in range(1, n_col)]

        def total(start, size):
            value = pf[c, col, :, start:start + size]
            for peer in peers:
                value = value + yrecv[c, peer, :, start:start + size].astype(jnp.float32)
            return value

        squares = pf[c, col, :, qo + nq:qo + nq + 1]
        for peer in peers:
            squares = squares + yrecv[c, peer, :, qo + nq:qo + nq + 1].astype(jnp.float32)
            squares = squares + yrecv[c, peer, :, qo + nq + 1:qo + nq + 2].astype(jnp.float32)
        factor = lax.rsqrt(squares / features + eps)
        q_ref[c] = (total(qo, nq) * factor).astype(jnp.bfloat16)
        gate = total(0, nf) * factor
        up = total(nf, nf) * factor
        h_ref[c] = (gate / (1.0 + jnp.exp(-gate)) * up).astype(jnp.bfloat16)

    stages = (s0, s1, s2, s3, s4, s5, s6, s7)

    def tick(t, carry):
        for s, run in enumerate(stages):
            at_stage(t, s, run)
        return carry

    lax.fori_loop(0, chunks + len(stages) - 1, tick, 0)

    def finish(c, carry):
        core_rs(c).wait_send()
        x_rs(c).wait_send()
        z_far_end(c).wait_send()

        @pl.when(inner)
        def _():
            z_near(c).wait_send()

        x_ag(c, q_own).wait_send()
        core_ag(c, q_own, 0).wait_send()
        core_ag(c, q_x, 1).wait_send()
        for d in range(1, n_col):
            y_send(c, d).wait_send()
        return carry

    lax.fori_loop(0, chunks, finish, 0)


def body(n_row, n_col, token_ids, table, norm_gain, w_qkv, w_gate, w_up):
    chunks = CHUNKS
    vocab_rows, dk = table.shape
    mine = token_ids.shape[0]
    rows = mine // chunks
    t4 = n_col * rows // 4
    nq, nf = w_qkv.shape[1], w_gate.shape[1]
    width = 2 * nf + (nq + 2 + 127) // 128 * 128
    every_id = lax.all_gather(token_ids, "col", axis=0, tiled=True)
    every_id = every_id.reshape(n_col, chunks, rows).transpose(1, 0, 2).reshape(-1)
    columns = lax.axis_index("row") * vocab_rows + lax.broadcasted_iota(jnp.int32, (1, vocab_rows), 1)
    onehot = (every_id[:, None] == columns).astype(jnp.bfloat16)
    part = jnp.dot(onehot, table, preferred_element_type=jnp.float32).astype(jnp.bfloat16)
    part = part.reshape(chunks, 4, t4, dk)
    bf = jnp.bfloat16
    dma = pltpu.SemaphoreType.DMA
    vmem = pl.BlockSpec(memory_space=pltpu.VMEM)
    hbm = pl.BlockSpec(memory_space=pl.ANY)
    q, h = pl.pallas_call(
        functools.partial(kernel, n_row, n_col, chunks, width, dk * n_col),
        out_shape=(
            jax.ShapeDtypeStruct((chunks, rows, nq), bf),
            jax.ShapeDtypeStruct((chunks, rows, nf), bf),
        ),
        in_specs=[vmem, vmem, hbm, hbm, hbm],
        out_specs=(vmem, vmem),
        scratch_shapes=[
            pltpu.VMEM(w_qkv.shape, bf),
            pltpu.VMEM(w_gate.shape, bf),
            pltpu.VMEM(w_up.shape, bf),
            pltpu.VMEM((chunks, 2, t4, dk), bf),
            pltpu.VMEM((chunks, t4, dk), bf),
            pltpu.VMEM((chunks, t4, dk), bf),
            pltpu.VMEM((chunks, t4, dk), bf),
            pltpu.VMEM((2, chunks, t4, dk), bf),
            pltpu.VMEM((chunks, t4, dk), bf),
            pltpu.VMEM((chunks, t4, dk), bf),
            pltpu.VMEM((chunks, 4, t4, dk), bf),
            pltpu.VMEM((4 * t4, dk), bf),
            pltpu.VMEM((chunks, n_col, rows, width), jnp.float32),
            pltpu.VMEM((chunks, n_col, rows, width), bf),
            pltpu.VMEM((chunks, n_col, rows, width), bf),
            dma((3,)),
            dma((chunks,)), dma((chunks,)),
            dma((chunks,)), dma((chunks,)),
            dma((chunks,)), dma((chunks,)), dma((2, chunks)),
            dma((chunks,)), dma((chunks,)),
            dma((chunks, 2)), dma((chunks, 2)),
            dma((chunks, max(n_col - 1, 1))), dma((chunks, n_col)),
        ],
        compiler_params=pltpu.CompilerParams(
            collective_id=0, has_side_effects=True, vmem_limit_bytes=56 * 1024 * 1024
        ),
    )(part, norm_gain.reshape(1, -1), w_qkv, w_gate, w_up)
    return q.reshape(mine, nq), h.reshape(mine, nf)


def solution(mesh):
    return jax.shard_map(
        functools.partial(body, mesh.shape["row"], mesh.shape["col"]),
        mesh=mesh,
        in_specs=(
            P("col"),
            P("row", "col"),
            P(),
            P("col", "row"),
            P("col", "row"),
            P("col", "row"),
        ),
        out_specs=(P("col", "row"), P("col", "row")),
        check_vma=False,
    )
```

```python
import functools

import jax
import jax.numpy as jnp
from jax import lax
from jax.experimental import pallas as pl
from jax.experimental.pallas import tpu as pltpu
from jax.sharding import PartitionSpec as P

eps = 1e-05
CHUNKS = 4
TILE = 256


def kernel(
    n_row, n_col, chunks, width, features,
    ids_ref, table_hbm, gain_ref, wq_hbm, wg_hbm, wu_hbm,
    q_ref, h_ref,
    tab, idbuf, onehot, part_ref, wq, wg, wu, crs, xsend, xrs, zown, zin, zfar_out, znear_out, act, xbuf, pf, ysend, yrecv,
    t_sem, id_s, id_r, w_sem, core_s, core_r, x_s, x_r, zf_s, zn_s, z_r, xa_s, xa_r, ca_s, ca_r, y_s, y_r,
):
    row = lax.axis_index("row")
    col = lax.axis_index("col")
    k = row % 2
    xx = (row // 2) % 2
    z = row // 4
    nz = n_row // 4
    upper = z // (nz // 2)
    sgn = 1 - 2 * upper
    core_peer = row + 1 - 2 * k
    x_peer = row + 2 - 4 * xx
    far_peer = row + 4 * sgn
    near_peer = row - 4 * sgn
    inner = jnp.logical_and(z > 0, z < nz - 1)
    q_own = 2 * k + xx
    q_x = 2 * k + 1 - xx
    q_c0 = 2 * (1 - k) + xx
    q_c1 = 2 * (1 - k) + 1 - xx
    near_slot, far_slot = upper, 1 - upper
    dk = part_ref.shape[3]
    t4 = part_ref.shape[2]
    nq, nf = wq.shape[0], wg.shape[1]
    qo = 2 * nf
    pieces = nf // TILE
    vocab = table_hbm.shape[0]
    n_tab, vocab_pad, tab_tile = tab.shape
    rows = ids_ref.shape[1]
    toks = n_col * rows

    w_copies = [
        pltpu.make_async_copy(wg_hbm, wg, w_sem.at[0]),
        pltpu.make_async_copy(wu_hbm, wu, w_sem.at[1]),
        pltpu.make_async_copy(wq_hbm, wq, w_sem.at[2]),
    ]

    def table_copy(i):
        return pltpu.make_async_copy(
            table_hbm.at[:, pl.ds(pl.multiple_of(i * tab_tile, 128), tab_tile)],
            tab.at[i, pl.ds(0, vocab)], t_sem.at[i],
        )

    clear = vocab // 16 * 16
    if vocab_pad > clear:
        tab[:, clear:, :] = jnp.zeros((n_tab, vocab_pad - clear, tab_tile), tab.dtype)
    for i in range(n_tab):
        table_copy(i).start()

    barrier = pltpu.get_barrier_semaphore()

    def greet(where):
        pl.semaphore_signal(barrier, inc=1, device_id=where, device_id_type=pl.DeviceIdType.MESH)

    greet({"row": core_peer})
    greet({"row": x_peer})
    greet({"row": far_peer})
    for d in range(1, n_col):
        greet({"col": (col + d) % n_col})

    @pl.when(inner)
    def _():
        greet({"row": near_peer})

    @pl.when(inner)
    def _():
        pl.semaphore_wait(barrier, 4 + n_col - 1)

    @pl.when(jnp.logical_not(inner))
    def _():
        pl.semaphore_wait(barrier, 3 + n_col - 1)

    def rcopy(src, dst, s, r, where):
        return pltpu.make_async_remote_copy(
            src_ref=src, dst_ref=dst, send_sem=s, recv_sem=r,
            device_id=where, device_id_type=pl.DeviceIdType.MESH,
        )

    def core_rs(c):
        return rcopy(part_ref.at[c, pl.ds(2 * (1 - k), 2)], crs.at[c], core_s.at[c], core_r.at[c], {"row": core_peer})

    def x_rs(c):
        return rcopy(xsend.at[c], xrs.at[c], x_s.at[c], x_r.at[c], {"row": x_peer})

    def z_far_end(c):
        return rcopy(zown.at[c], zin.at[upper, c], zf_s.at[c], z_r.at[upper, c], {"row": far_peer})

    def z_far_inner(c):
        return rcopy(zfar_out.at[c], zin.at[upper, c], zf_s.at[c], z_r.at[upper, c], {"row": far_peer})

    def z_near(c):
        return rcopy(znear_out.at[c], zin.at[1 - upper, c], zn_s.at[c], z_r.at[1 - upper, c], {"row": near_peer})

    def z_wait(slot, c):
        rcopy(zown.at[c], zin.at[slot, c], zf_s.at[c], z_r.at[slot, c], {"row": far_peer}).wait_recv()

    def x_ag(c, q):
        return rcopy(act.at[c, q], act.at[c, q], xa_s.at[c], xa_r.at[c], {"row": x_peer})

    def core_ag(c, q, i):
        return rcopy(act.at[c, q], act.at[c, q], ca_s.at[c, i], ca_r.at[c, i], {"row": core_peer})

    def id_send(d):
        peer = (col + d) % n_col
        return rcopy(ids_ref, idbuf.at[col], id_s.at[d - 1], id_r.at[col], {"col": peer})

    def id_wait(d):
        peer = (col + d) % n_col
        rcopy(ids_ref, idbuf.at[peer], id_s.at[d - 1], id_r.at[peer], {"col": peer}).wait_recv()

    for d in range(1, n_col):
        id_send(d).start()

    def y_lanes(j):
        if isinstance(j, int) and j == pieces:
            return pl.ds(qo, width - qo)
        return pl.ds(pl.multiple_of(j * 2 * TILE, 128), 2 * TILE)

    def y_copy(c, d, j, slot):
        peer = (col + d) % n_col
        at = y_lanes(j)
        return rcopy(
            ysend.at[c, peer, :, at], yrecv.at[c, slot, :, at],
            y_s.at[c, d - 1, j], y_r.at[c, slot, j], {"col": peer},
        )

    def y_send(c, d, j):
        return y_copy(c, d, j, col)

    def y_wait(c, j):
        for d in range(1, n_col):
            y_copy(c, d, j, (col + d) % n_col).wait_recv()

    def at_stage(t, s, run):
        c = t - s

        @pl.when(jnp.logical_and(c >= 0, c < chunks))
        def _():
            run(c)

    def s0(c):
        @pl.when(c == 0)
        def _():
            for d in range(1, n_col):
                id_wait(d)

        base = row * vocab
        lane = lax.broadcasted_iota(jnp.int32, (rows, 128), 1)
        for d in range(n_col):
            at = (col + d) % n_col
            local = (ids_ref[c] if d == 0 else idbuf[at, c]) - base - lane
            for i in range(vocab_pad // 128):
                hit = jnp.where(local == i * 128, 1.0, 0.0).astype(jnp.bfloat16)
                onehot[at, :, i * 128:(i + 1) * 128] = hit

        def columns(i, carry):
            @pl.when(c == 0)
            def _():
                table_copy(i).wait()

            found = jnp.dot(onehot[...].reshape(toks, vocab_pad), tab[i], preferred_element_type=jnp.float32)
            at = pl.ds(pl.multiple_of(i * tab_tile, 128), tab_tile)
            part_ref[c, :, :, at] = found.astype(jnp.bfloat16).reshape(4, t4, tab_tile)
            return carry

        lax.fori_loop(0, n_tab, columns, 0)
        core_rs(c).start()

        @pl.when(c == 0)
        def _():
            for copy in w_copies:
                copy.start()

    def s1(c):
        core_rs(c).wait_recv()
        xsend[c] = part_ref[c, q_x] + crs[c, 1 - xx]
        x_rs(c).start()
        zown[c] = part_ref[c, q_own] + crs[c, xx]

    def s2(c):
        x_rs(c).wait_recv()
        zown[c] = zown[c] + xrs[c]

        @pl.when(jnp.logical_not(inner))
        def _():
            z_far_end(c).start()

    def s3(c):
        @pl.when(inner)
        def _():
            z_wait(near_slot, c)
            zfar_out[c] = zown[c] + zin[near_slot, c]
            z_far_inner(c).start()

    def s4(c):
        z_wait(far_slot, c)

        @pl.when(inner)
        def _():
            znear_out[c] = zown[c] + zin[far_slot, c]
            z_near(c).start()
            act[c, q_own] = zfar_out[c] + zin[far_slot, c]

        @pl.when(jnp.logical_not(inner))
        def _():
            act[c, q_own] = zown[c] + zin[far_slot, c]

        x_ag(c, q_own).start()
        core_ag(c, q_own, 0).start()

    def s5(c):
        x_ag(c, q_x).wait_recv()
        core_ag(c, q_x, 1).start()

    def s6(c):
        core_ag(c, q_c0, 0).wait_recv()
        core_ag(c, q_c1, 1).wait_recv()

        @pl.when(c == 0)
        def _():
            for copy in w_copies:
                copy.wait()

        gain = gain_ref[:, pl.ds(pl.multiple_of(col * dk, 128), dk)]
        values = act[c].reshape(toks, dk).astype(jnp.float32)
        squares = jnp.sum(values * values, axis=1, keepdims=True)
        xbuf[...] = (values * gain).astype(jnp.bfloat16)
        high = squares.astype(jnp.bfloat16)
        low = (squares - high.astype(jnp.float32)).astype(jnp.bfloat16)
        tail = width - qo - nq
        lane = lax.broadcasted_iota(jnp.int32, (toks, tail), 1)
        pf[c, :, :, qo + nq:] = jnp.broadcast_to(squares, (toks, tail)).reshape(n_col, rows, tail)
        both = jnp.where(lane == 0, high.astype(jnp.float32), low.astype(jnp.float32)).astype(jnp.bfloat16)
        ysend[c, :, :, qo + nq:] = both.reshape(n_col, rows, tail)

        def put(start, out, size):
            out = out.reshape(n_col, rows, size)
            pf[c, :, :, pl.ds(start, size)] = out
            ysend[c, :, :, pl.ds(start, size)] = out.astype(jnp.bfloat16)

        put(
            qo,
            lax.dot_general(xbuf[...], wq[...], (((1,), (1,)), ((), ())), preferred_element_type=jnp.float32), nq,
        )
        for d in range(1, n_col):
            y_send(c, d, pieces).start()

        def tiles(j, carry):
            at = pl.ds(pl.multiple_of(j * TILE, TILE), TILE)
            start = pl.multiple_of(2 * j * TILE, TILE)
            put(start, jnp.dot(xbuf[...], wg[:, at], preferred_element_type=jnp.float32), TILE)
            put(
                pl.multiple_of(start + TILE, TILE),
                jnp.dot(xbuf[...], wu[:, at], preferred_element_type=jnp.float32), TILE,
            )
            for d in range(1, n_col):
                y_send(c, d, j).start()
            return carry

        lax.fori_loop(0, pieces, tiles, 0)

    def s7(c):
        peers = [(col + d) % n_col for d in range(1, n_col)]

        def total(start, size):
            at = pl.ds(start, size)
            value = pf[c, col, :, at]
            for peer in peers:
                value = value + yrecv[c, peer, :, at].astype(jnp.float32)
            return value

        y_wait(c, pieces)
        squares = pf[c, col, :, qo + nq:qo + nq + 1]
        for peer in peers:
            squares = squares + yrecv[c, peer, :, qo + nq:qo + nq + 1].astype(jnp.float32)
            squares = squares + yrecv[c, peer, :, qo + nq + 1:qo + nq + 2].astype(jnp.float32)
        factor = lax.rsqrt(squares / features + eps)
        q_ref[c] = (total(qo, nq) * factor).astype(jnp.bfloat16)

        def tiles(j, carry):
            y_wait(c, j)
            start = pl.multiple_of(2 * j * TILE, TILE)
            gate = total(start, TILE) * factor
            up = total(pl.multiple_of(start + TILE, TILE), TILE) * factor
            at = pl.ds(pl.multiple_of(j * TILE, TILE), TILE)
            h_ref[c, :, at] = (gate / (1.0 + jnp.exp(-gate)) * up).astype(jnp.bfloat16)
            return carry

        lax.fori_loop(0, pieces, tiles, 0)

    stages = ((1, s1), (2, s2), (3, s3), (4, s4), (5, s5), (0, s0), (6, s6), (7, s7))

    def tick(t, carry):
        for s, run in stages:
            at_stage(t, s, run)
        return carry

    lax.fori_loop(0, chunks + len(stages) - 1, tick, 0)

    def finish(c, carry):
        core_rs(c).wait_send()
        x_rs(c).wait_send()
        z_far_end(c).wait_send()

        @pl.when(inner)
        def _():
            z_near(c).wait_send()

        x_ag(c, q_own).wait_send()
        core_ag(c, q_own, 0).wait_send()
        core_ag(c, q_x, 1).wait_send()
        for d in range(1, n_col):
            for j in range(pieces + 1):
                y_send(c, d, j).wait_send()
        return carry

    lax.fori_loop(0, chunks, finish, 0)
    for d in range(1, n_col):
        id_send(d).wait_send()


def body(n_row, n_col, token_ids, table, norm_gain, w_qkv, w_gate, w_up):
    chunks = CHUNKS
    vocab_rows, dk = table.shape
    mine = token_ids.shape[0]
    rows = mine // chunks
    t4 = n_col * rows // 4
    nq, nf = w_qkv.shape[1], w_gate.shape[1]
    width = 2 * nf + (nq + 2 + 127) // 128 * 128
    ids = jnp.broadcast_to(token_ids.reshape(chunks, rows, 1), (chunks, rows, 128))
    tab_tile = 512 if dk % 512 == 0 else 128
    n_tab = dk // tab_tile
    vocab_pad = (vocab_rows + 127) // 128 * 128
    pieces = nf // TILE
    bf = jnp.bfloat16
    dma = pltpu.SemaphoreType.DMA
    vmem = pl.BlockSpec(memory_space=pltpu.VMEM)
    hbm = pl.BlockSpec(memory_space=pl.ANY)
    q, h = pl.pallas_call(
        functools.partial(kernel, n_row, n_col, chunks, width, dk * n_col),
        out_shape=(
            jax.ShapeDtypeStruct((chunks, rows, nq), bf),
            jax.ShapeDtypeStruct((chunks, rows, nf), bf),
        ),
        in_specs=[vmem, hbm, vmem, hbm, hbm, hbm],
        out_specs=(vmem, vmem),
        scratch_shapes=[
            pltpu.VMEM((n_tab, vocab_pad, tab_tile), bf),
            pltpu.VMEM((n_col, chunks, rows, 128), jnp.int32),
            pltpu.VMEM((n_col, rows, vocab_pad), bf),
            pltpu.VMEM((chunks, 4, t4, dk), bf),
            pltpu.VMEM((nq, dk), bf),
            pltpu.VMEM(w_gate.shape, bf),
            pltpu.VMEM(w_up.shape, bf),
            pltpu.VMEM((chunks, 2, t4, dk), bf),
            pltpu.VMEM((chunks, t4, dk), bf),
            pltpu.VMEM((chunks, t4, dk), bf),
            pltpu.VMEM((chunks, t4, dk), bf),
            pltpu.VMEM((2, chunks, t4, dk), bf),
            pltpu.VMEM((chunks, t4, dk), bf),
            pltpu.VMEM((chunks, t4, dk), bf),
            pltpu.VMEM((chunks, 4, t4, dk), bf),
            pltpu.VMEM((4 * t4, dk), bf),
            pltpu.VMEM((chunks, n_col, rows, width), jnp.float32),
            pltpu.VMEM((chunks, n_col, rows, width), bf),
            pltpu.VMEM((chunks, n_col, rows, width), bf),
            dma((n_tab,)), dma((max(n_col - 1, 1),)), dma((n_col,)),
            dma((3,)),
            dma((chunks,)), dma((chunks,)),
            dma((chunks,)), dma((chunks,)),
            dma((chunks,)), dma((chunks,)), dma((2, chunks)),
            dma((chunks,)), dma((chunks,)),
            dma((chunks, 2)), dma((chunks, 2)),
            dma((chunks, max(n_col - 1, 1), pieces + 1)), dma((chunks, n_col, pieces + 1)),
        ],
        compiler_params=pltpu.CompilerParams(
            collective_id=0, has_side_effects=True, vmem_limit_bytes=62 * 1024 * 1024
        ),
    )(ids, table, norm_gain.reshape(1, -1), w_qkv.T, w_gate, w_up)
    return q.reshape(mine, nq), h.reshape(mine, nf)


def solution(mesh):
    return jax.shard_map(
        functools.partial(body, mesh.shape["row"], mesh.shape["col"]),
        mesh=mesh,
        in_specs=(
            P("col"),
            P("row", "col"),
            P(),
            P("col", "row"),
            P("col", "row"),
            P("col", "row"),
        ),
        out_specs=(P("col", "row"), P("col", "row")),
        check_vma=False,
    )
```

```python
import functools

import jax
import jax.numpy as jnp
from jax import lax
from jax.experimental import pallas as pl
from jax.experimental.pallas import tpu as pltpu
from jax.sharding import PartitionSpec as P

eps = 1e-05
BLOCKS = 4
TILE = 256


def kernel(
    n_row, n_col, blocks, width, features,
    ids_ref, table_hbm, gain_ref, wq_hbm, wg_hbm, wu_hbm,
    q_ref, h_ref,
    tab, idbuf, onehot, part_ref, wq, wg, wu, crs, xsend, xrs, zown, zin, zfar_out, znear_out, act, xbuf, pf, ysend, yrecv,
    t_sem, id_s, id_r, w_sem, core_s, core_r, x_s, x_r, zf_s, zn_s, z_r, xa_s, xa_r, ca_s, ca_r, y_s, y_r,
):
    row = lax.axis_index("row")
    col = lax.axis_index("col")
    k = row % 2
    xx = (row // 2) % 2
    z = row // 4
    nz = n_row // 4
    upper = z // (nz // 2)
    sgn = 1 - 2 * upper
    core_peer = row + 1 - 2 * k
    x_peer = row + 2 - 4 * xx
    far_peer = row + 4 * sgn
    near_peer = row - 4 * sgn
    inner = jnp.logical_and(z > 0, z < nz - 1)
    q_own = 2 * k + xx
    q_x = 2 * k + 1 - xx
    q_c0 = 2 * (1 - k) + xx
    q_c1 = 2 * (1 - k) + 1 - xx
    near_slot, far_slot = upper, 1 - upper
    dk = part_ref.shape[3]
    t4 = part_ref.shape[2]
    nq, nf = wq.shape[0], wg.shape[1]
    qo = 2 * nf
    pieces = nf // TILE
    vocab = table_hbm.shape[0]
    n_tab, vocab_pad, tab_tile = tab.shape
    rows = ids_ref.shape[1]
    toks = n_col * rows
    chunks = 2 * blocks
    half_tab, half_pieces = n_tab // 2, pieces // 2

    w_copies = [
        pltpu.make_async_copy(wg_hbm, wg, w_sem.at[0]),
        pltpu.make_async_copy(wu_hbm, wu, w_sem.at[1]),
        pltpu.make_async_copy(wq_hbm, wq, w_sem.at[2]),
    ]

    def table_copy(i):
        return pltpu.make_async_copy(
            table_hbm.at[:, pl.ds(pl.multiple_of(i * tab_tile, 128), tab_tile)],
            tab.at[i, pl.ds(0, vocab)], t_sem.at[i],
        )

    clear = vocab // 16 * 16
    if vocab_pad > clear:
        tab[:, clear:, :] = jnp.zeros((n_tab, vocab_pad - clear, tab_tile), tab.dtype)
    for i in range(n_tab):
        table_copy(i).start()

    barrier = pltpu.get_barrier_semaphore()

    def greet(where):
        pl.semaphore_signal(barrier, inc=1, device_id=where, device_id_type=pl.DeviceIdType.MESH)

    greet({"row": core_peer})
    greet({"row": x_peer})
    greet({"row": far_peer})
    for d in range(1, n_col):
        greet({"col": (col + d) % n_col})

    @pl.when(inner)
    def _():
        greet({"row": near_peer})

    @pl.when(inner)
    def _():
        pl.semaphore_wait(barrier, 4 + n_col - 1)

    @pl.when(jnp.logical_not(inner))
    def _():
        pl.semaphore_wait(barrier, 3 + n_col - 1)

    def rcopy(src, dst, s, r, where):
        return pltpu.make_async_remote_copy(
            src_ref=src, dst_ref=dst, send_sem=s, recv_sem=r,
            device_id=where, device_id_type=pl.DeviceIdType.MESH,
        )

    def core_rs(c):
        return rcopy(part_ref.at[c, pl.ds(2 * (1 - k), 2)], crs.at[c], core_s.at[c], core_r.at[c], {"row": core_peer})

    def x_rs(c):
        return rcopy(xsend.at[c], xrs.at[c], x_s.at[c], x_r.at[c], {"row": x_peer})

    def z_far_end(c):
        return rcopy(zown.at[c], zin.at[upper, c], zf_s.at[c], z_r.at[upper, c], {"row": far_peer})

    def z_far_inner(c):
        return rcopy(zfar_out.at[c], zin.at[upper, c], zf_s.at[c], z_r.at[upper, c], {"row": far_peer})

    def z_near(c):
        return rcopy(znear_out.at[c], zin.at[1 - upper, c], zn_s.at[c], z_r.at[1 - upper, c], {"row": near_peer})

    def z_wait(slot, c):
        rcopy(zown.at[c], zin.at[slot, c], zf_s.at[c], z_r.at[slot, c], {"row": far_peer}).wait_recv()

    def x_ag(c, q):
        return rcopy(act.at[c, q], act.at[c, q], xa_s.at[c], xa_r.at[c], {"row": x_peer})

    def core_ag(c, q, i):
        return rcopy(act.at[c, q], act.at[c, q], ca_s.at[c, i], ca_r.at[c, i], {"row": core_peer})

    def id_send(d):
        peer = (col + d) % n_col
        return rcopy(ids_ref, idbuf.at[col], id_s.at[d - 1], id_r.at[col], {"col": peer})

    def id_wait(d):
        peer = (col + d) % n_col
        rcopy(ids_ref, idbuf.at[peer], id_s.at[d - 1], id_r.at[peer], {"col": peer}).wait_recv()

    for d in range(1, n_col):
        id_send(d).start()

    def y_lanes(j):
        if isinstance(j, int) and j == pieces:
            return pl.ds(qo, width - qo)
        return pl.ds(pl.multiple_of(j * 2 * TILE, 128), 2 * TILE)

    def y_copy(c, d, j, slot):
        peer = (col + d) % n_col
        at = y_lanes(j)
        return rcopy(
            ysend.at[c, peer, :, at], yrecv.at[c, slot, :, at],
            y_s.at[c, d - 1, j], y_r.at[c, slot, j], {"col": peer},
        )

    def y_send(c, d, j):
        return y_copy(c, d, j, col)

    def y_wait(c, j):
        for d in range(1, n_col):
            y_copy(c, d, j, (col + d) % n_col).wait_recv()

    def at_stage(t, s, run):
        c = t - s

        @pl.when(jnp.logical_and(c >= 0, c < chunks))
        def _():
            run(c)

    def fill_onehot(b):
        base = row * vocab
        lane = lax.broadcasted_iota(jnp.int32, (rows, 128), 1)
        for d in range(n_col):
            at = (col + d) % n_col
            local = (ids_ref[b] if d == 0 else idbuf[at, b]) - base - lane
            for i in range(vocab_pad // 128):
                hit = jnp.where(local == i * 128, 1.0, 0.0).astype(jnp.bfloat16)
                onehot[at, :, i * 128:(i + 1) * 128] = hit

    def lookup(t):
        odd = t % 2
        b = (t + 1) // 2

        @pl.when(t == 0)
        def _():
            for d in range(1, n_col):
                id_wait(d)

        @pl.when(jnp.logical_or(t == 0, odd == 1))
        def _():
            fill_onehot(b)

        def columns(i, carry):
            @pl.when(t == 0)
            def _():
                table_copy(i).wait()

            found = jnp.dot(onehot[...].reshape(toks, vocab_pad), tab[i], preferred_element_type=jnp.float32)
            at = pl.ds(pl.multiple_of(i * tab_tile, 128), tab_tile)
            part_ref[pl.ds(2 * b, 2), :, :, at] = found.astype(jnp.bfloat16).reshape(2, 4, t4, tab_tile)
            return carry

        first = (1 - odd) * jnp.minimum(t, 1) * half_tab
        lax.fori_loop(first, odd * half_tab + (1 - odd) * n_tab, columns, 0)

        @pl.when(odd == 0)
        def _():
            core_rs(t).start()
            core_rs(t + 1).start()

        @pl.when(t == 0)
        def _():
            for copy in w_copies:
                copy.start()

    def s1(c):
        core_rs(c).wait_recv()
        xsend[c] = part_ref[c, q_x] + crs[c, 1 - xx]
        x_rs(c).start()
        zown[c] = part_ref[c, q_own] + crs[c, xx]

    def s2(c):
        x_rs(c).wait_recv()
        zown[c] = zown[c] + xrs[c]

        @pl.when(jnp.logical_not(inner))
        def _():
            z_far_end(c).start()

    def s3(c):
        @pl.when(inner)
        def _():
            z_wait(near_slot, c)
            zfar_out[c] = zown[c] + zin[near_slot, c]
            z_far_inner(c).start()

    def s4(c):
        z_wait(far_slot, c)

        @pl.when(inner)
        def _():
            znear_out[c] = zown[c] + zin[far_slot, c]
            z_near(c).start()
            act[c, q_own] = zfar_out[c] + zin[far_slot, c]

        @pl.when(jnp.logical_not(inner))
        def _():
            act[c, q_own] = zown[c] + zin[far_slot, c]

        x_ag(c, q_own).start()
        core_ag(c, q_own, 0).start()

    def s5(c):
        x_ag(c, q_x).wait_recv()
        core_ag(c, q_x, 1).start()

    def put(c, start, out, size):
        out = out.reshape(n_col, rows, size)
        pf[c, :, :, pl.ds(start, size)] = out
        ysend[c, :, :, pl.ds(start, size)] = out.astype(jnp.bfloat16)

    def prepare(c):
        for i in range(2):
            core_ag(2 * c + i, q_c0, 0).wait_recv()
            core_ag(2 * c + i, q_c1, 1).wait_recv()

        @pl.when(c == 0)
        def _():
            for copy in w_copies:
                copy.wait()

        gain = gain_ref[:, pl.ds(pl.multiple_of(col * dk, 128), dk)]
        values = act[pl.ds(2 * c, 2)].reshape(toks, dk).astype(jnp.float32)
        squares = jnp.sum(values * values, axis=1, keepdims=True)
        xbuf[...] = (values * gain).astype(jnp.bfloat16)
        high = squares.astype(jnp.bfloat16)
        low = (squares - high.astype(jnp.float32)).astype(jnp.bfloat16)
        tail = width - qo - nq
        lane = lax.broadcasted_iota(jnp.int32, (toks, tail), 1)
        pf[c, :, :, qo + nq:] = jnp.broadcast_to(squares, (toks, tail)).reshape(n_col, rows, tail)
        both = jnp.where(lane == 0, high.astype(jnp.float32), low.astype(jnp.float32)).astype(jnp.bfloat16)
        ysend[c, :, :, qo + nq:] = both.reshape(n_col, rows, tail)

        put(
            c, qo,
            lax.dot_general(xbuf[...], wq[...], (((1,), (1,)), ((), ())), preferred_element_type=jnp.float32), nq,
        )
        for d in range(1, n_col):
            y_send(c, d, pieces).start()

    def products(c, first, last):
        def tiles(j, carry):
            at = pl.ds(pl.multiple_of(j * TILE, TILE), TILE)
            start = pl.multiple_of(2 * j * TILE, TILE)
            put(c, start, jnp.dot(xbuf[...], wg[:, at], preferred_element_type=jnp.float32), TILE)
            put(
                c, pl.multiple_of(start + TILE, TILE),
                jnp.dot(xbuf[...], wu[:, at], preferred_element_type=jnp.float32), TILE,
            )
            for d in range(1, n_col):
                y_send(c, d, j).start()
            return carry

        lax.fori_loop(first, last, tiles, 0)

    def s7(c):
        peers = [(col + d) % n_col for d in range(1, n_col)]

        def total(start, size):
            at = pl.ds(start, size)
            value = pf[c, col, :, at]
            for peer in peers:
                value = value + yrecv[c, peer, :, at].astype(jnp.float32)
            return value

        y_wait(c, pieces)
        squares = pf[c, col, :, qo + nq:qo + nq + 1]
        for peer in peers:
            squares = squares + yrecv[c, peer, :, qo + nq:qo + nq + 1].astype(jnp.float32)
            squares = squares + yrecv[c, peer, :, qo + nq + 1:qo + nq + 2].astype(jnp.float32)
        factor = lax.rsqrt(squares / features + eps)
        q_ref[c] = (total(qo, nq) * factor).astype(jnp.bfloat16)

        def tiles(j, carry):
            y_wait(c, j)
            start = pl.multiple_of(2 * j * TILE, TILE)
            gate = total(start, TILE) * factor
            up = total(pl.multiple_of(start + TILE, TILE), TILE) * factor
            at = pl.ds(pl.multiple_of(j * TILE, TILE), TILE)
            h_ref[c, :, at] = (gate / (1.0 + jnp.exp(-gate)) * up).astype(jnp.bfloat16)
            return carry

        lax.fori_loop(0, pieces, tiles, 0)

    stages = ((1, s1), (2, s2), (3, s3), (4, s4), (5, s5))

    def tick(t, carry):
        for s, run in stages:
            at_stage(t, s, run)

        @pl.when(t < chunks - 1)
        def _():
            lookup(t)

        since = t - 7
        b = (t - 7) // 2

        @pl.when(jnp.logical_and(since >= 0, since < chunks))
        def _():
            odd = since % 2

            @pl.when(odd == 0)
            def _():
                prepare(b)

            products(b, odd * half_pieces, (1 - odd) * half_pieces + odd * pieces)

            @pl.when(odd == 1)
            def _():
                s7(b)
        return carry

    lax.fori_loop(0, chunks + 7, tick, 0)

    def finish(c, carry):
        core_rs(c).wait_send()
        x_rs(c).wait_send()
        z_far_end(c).wait_send()

        @pl.when(inner)
        def _():
            z_near(c).wait_send()

        x_ag(c, q_own).wait_send()
        core_ag(c, q_own, 0).wait_send()
        core_ag(c, q_x, 1).wait_send()
        return carry

    def finish_y(c, carry):
        for d in range(1, n_col):
            for j in range(pieces + 1):
                y_send(c, d, j).wait_send()
        return carry

    lax.fori_loop(0, chunks, finish, 0)
    lax.fori_loop(0, blocks, finish_y, 0)
    for d in range(1, n_col):
        id_send(d).wait_send()


def body(n_row, n_col, token_ids, table, norm_gain, w_qkv, w_gate, w_up):
    blocks = BLOCKS
    chunks = 2 * blocks
    vocab_rows, dk = table.shape
    mine = token_ids.shape[0]
    rows = mine // blocks
    t4 = n_col * rows // 8
    nq, nf = w_qkv.shape[1], w_gate.shape[1]
    width = 2 * nf + (nq + 2 + 127) // 128 * 128
    ids = jnp.broadcast_to(token_ids.reshape(blocks, rows, 1), (blocks, rows, 128))
    tab_tile = 256 if dk % 256 == 0 else 128
    n_tab = dk // tab_tile
    vocab_pad = (vocab_rows + 127) // 128 * 128
    pieces = nf // TILE
    bf = jnp.bfloat16
    dma = pltpu.SemaphoreType.DMA
    vmem = pl.BlockSpec(memory_space=pltpu.VMEM)
    hbm = pl.BlockSpec(memory_space=pl.ANY)
    q, h = pl.pallas_call(
        functools.partial(kernel, n_row, n_col, blocks, width, dk * n_col),
        out_shape=(
            jax.ShapeDtypeStruct((blocks, rows, nq), bf),
            jax.ShapeDtypeStruct((blocks, rows, nf), bf),
        ),
        in_specs=[vmem, hbm, vmem, hbm, hbm, hbm],
        out_specs=(vmem, vmem),
        scratch_shapes=[
            pltpu.VMEM((n_tab, vocab_pad, tab_tile), bf),
            pltpu.VMEM((n_col, blocks, rows, 128), jnp.int32),
            pltpu.VMEM((n_col, rows, vocab_pad), bf),
            pltpu.VMEM((chunks, 4, t4, dk), bf),
            pltpu.VMEM((nq, dk), bf),
            pltpu.VMEM(w_gate.shape, bf),
            pltpu.VMEM(w_up.shape, bf),
            pltpu.VMEM((chunks, 2, t4, dk), bf),
            pltpu.VMEM((chunks, t4, dk), bf),
            pltpu.VMEM((chunks, t4, dk), bf),
            pltpu.VMEM((chunks, t4, dk), bf),
            pltpu.VMEM((2, chunks, t4, dk), bf),
            pltpu.VMEM((chunks, t4, dk), bf),
            pltpu.VMEM((chunks, t4, dk), bf),
            pltpu.VMEM((chunks, 4, t4, dk), bf),
            pltpu.VMEM((n_col * rows, dk), bf),
            pltpu.VMEM((blocks, n_col, rows, width), jnp.float32),
            pltpu.VMEM((blocks, n_col, rows, width), bf),
            pltpu.VMEM((blocks, n_col, rows, width), bf),
            dma((n_tab,)), dma((max(n_col - 1, 1),)), dma((n_col,)),
            dma((3,)),
            dma((chunks,)), dma((chunks,)),
            dma((chunks,)), dma((chunks,)),
            dma((chunks,)), dma((chunks,)), dma((2, chunks)),
            dma((chunks,)), dma((chunks,)),
            dma((chunks, 2)), dma((chunks, 2)),
            dma((blocks, max(n_col - 1, 1), pieces + 1)), dma((blocks, n_col, pieces + 1)),
        ],
        compiler_params=pltpu.CompilerParams(
            collective_id=0, has_side_effects=True, vmem_limit_bytes=62 * 1024 * 1024
        ),
    )(ids, table, norm_gain.reshape(1, -1), w_qkv.T, w_gate, w_up)
    return q.reshape(mine, nq), h.reshape(mine, nf)


def solution(mesh):
    return jax.shard_map(
        functools.partial(body, mesh.shape["row"], mesh.shape["col"]),
        mesh=mesh,
        in_specs=(
            P("col"),
            P("row", "col"),
            P(),
            P("col", "row"),
            P("col", "row"),
            P("col", "row"),
        ),
        out_specs=(P("col", "row"), P("col", "row")),
        check_vma=False,
    )
```

```python
import functools

import jax
import jax.numpy as jnp
from jax import lax
from jax.experimental import pallas as pl
from jax.experimental.pallas import tpu as pltpu
from jax.sharding import PartitionSpec as P

eps = 1e-05
CHUNKS = 4
TILE = 256


def kernel(
    n_row, n_col, chunks, width, features,
    ids_ref, table_hbm, gain_ref, wq_hbm, wg_hbm, wu_hbm,
    q_ref, h_ref,
    tab, idbuf, onehot, part_ref, wq, wg, wu, crs, xsend, xrs, zown, zin, zfar_out, znear_out, act, xbuf, pf, ysend, yrecv,
    t_sem, id_s, id_r, w_sem, core_s, core_r, x_s, x_r, zf_s, zn_s, z_r, xa_s, xa_r, ca_s, ca_r, y_s, y_r,
):
    row = lax.axis_index("row")
    col = lax.axis_index("col")
    k = row % 2
    xx = (row // 2) % 2
    z = row // 4
    nz = n_row // 4
    upper = z // (nz // 2)
    sgn = 1 - 2 * upper
    core_peer = row + 1 - 2 * k
    x_peer = row + 2 - 4 * xx
    far_peer = row + 4 * sgn
    near_peer = row - 4 * sgn
    inner = jnp.logical_and(z > 0, z < nz - 1)
    q_own = 2 * k + xx
    q_x = 2 * k + 1 - xx
    q_c0 = 2 * (1 - k) + xx
    q_c1 = 2 * (1 - k) + 1 - xx
    near_slot, far_slot = upper, 1 - upper
    dk = part_ref.shape[3]
    t4 = part_ref.shape[2]
    nq, nf = wq.shape[0], wg.shape[1]
    qo = 2 * nf
    pieces = nf // TILE
    vocab = table_hbm.shape[0]
    n_tab, vocab_pad, tab_tile = tab.shape
    rows = ids_ref.shape[2]
    toks = n_col * rows

    w_copies = [
        pltpu.make_async_copy(wg_hbm, wg, w_sem.at[0]),
        pltpu.make_async_copy(wu_hbm, wu, w_sem.at[1]),
        pltpu.make_async_copy(wq_hbm, wq, w_sem.at[2]),
    ]

    def table_copy(i):
        return pltpu.make_async_copy(
            table_hbm.at[:, pl.ds(pl.multiple_of(i * tab_tile, 128), tab_tile)],
            tab.at[i, pl.ds(0, vocab)], t_sem.at[i],
        )

    clear = vocab // 16 * 16
    if vocab_pad > clear:
        tab[:, clear:, :] = jnp.zeros((n_tab, vocab_pad - clear, tab_tile), tab.dtype)
    for i in range(n_tab):
        table_copy(i).start()

    barrier = pltpu.get_barrier_semaphore()

    def greet(where):
        pl.semaphore_signal(barrier, inc=1, device_id=where, device_id_type=pl.DeviceIdType.MESH)

    greet({"row": core_peer})
    greet({"row": x_peer})
    greet({"row": far_peer})
    for d in range(1, n_col):
        greet({"col": (col + d) % n_col})

    @pl.when(inner)
    def _():
        greet({"row": near_peer})

    @pl.when(inner)
    def _():
        pl.semaphore_wait(barrier, 4 + n_col - 1)

    @pl.when(jnp.logical_not(inner))
    def _():
        pl.semaphore_wait(barrier, 3 + n_col - 1)

    def rcopy(src, dst, s, r, where):
        return pltpu.make_async_remote_copy(
            src_ref=src, dst_ref=dst, send_sem=s, recv_sem=r,
            device_id=where, device_id_type=pl.DeviceIdType.MESH,
        )

    def core_rs(c):
        return rcopy(part_ref.at[c, pl.ds(2 * (1 - k), 2)], crs.at[c], core_s.at[c], core_r.at[c], {"row": core_peer})

    def x_rs(c):
        return rcopy(xsend.at[c], xrs.at[c], x_s.at[c], x_r.at[c], {"row": x_peer})

    def z_far_end(c):
        return rcopy(zown.at[c], zin.at[upper, c], zf_s.at[c], z_r.at[upper, c], {"row": far_peer})

    def z_far_inner(c):
        return rcopy(zfar_out.at[c], zin.at[upper, c], zf_s.at[c], z_r.at[upper, c], {"row": far_peer})

    def z_near(c):
        return rcopy(znear_out.at[c], zin.at[1 - upper, c], zn_s.at[c], z_r.at[1 - upper, c], {"row": near_peer})

    def z_wait(slot, c):
        rcopy(zown.at[c], zin.at[slot, c], zf_s.at[c], z_r.at[slot, c], {"row": far_peer}).wait_recv()

    def x_ag(c, q):
        return rcopy(act.at[c, q], act.at[c, q], xa_s.at[c], xa_r.at[c], {"row": x_peer})

    def core_ag(c, q, i):
        return rcopy(act.at[c, q], act.at[c, q], ca_s.at[c, i], ca_r.at[c, i], {"row": core_peer})

    def id_send(d):
        peer = (col + d) % n_col
        return rcopy(ids_ref, idbuf.at[col], id_s.at[d - 1], id_r.at[col], {"col": peer})

    def id_wait(d):
        peer = (col + d) % n_col
        rcopy(ids_ref, idbuf.at[peer], id_s.at[d - 1], id_r.at[peer], {"col": peer}).wait_recv()

    for d in range(1, n_col):
        id_send(d).start()

    def y_lanes(j):
        if isinstance(j, int) and j == pieces:
            return pl.ds(qo, width - qo)
        return pl.ds(pl.multiple_of(j * 2 * TILE, 128), 2 * TILE)

    def y_copy(c, d, j, slot):
        peer = (col + d) % n_col
        at = y_lanes(j)
        return rcopy(
            ysend.at[c, peer, :, at], yrecv.at[c, slot, :, at],
            y_s.at[c, d - 1, j], y_r.at[c, slot, j], {"col": peer},
        )

    def y_send(c, d, j):
        return y_copy(c, d, j, col)

    def y_wait(c, j):
        for d in range(1, n_col):
            y_copy(c, d, j, (col + d) % n_col).wait_recv()

    def at_stage(t, s, run):
        c = t - s

        @pl.when(jnp.logical_and(c >= 0, c < chunks))
        def _():
            run(c)

    def s0(c):
        @pl.when(c == 0)
        def _():
            for d in range(1, n_col):
                id_wait(d)

        base = row * vocab
        lane = lax.broadcasted_iota(jnp.int32, (rows, 128), 1)
        for d in range(n_col):
            at = (col + d) % n_col
            line = ids_ref[c] if d == 0 else idbuf[at, c]
            local = jnp.transpose(jnp.broadcast_to(line, (128, rows))) - base - lane
            for i in range(vocab_pad // 128):
                hit = jnp.where(local == i * 128, 1.0, 0.0).astype(jnp.bfloat16)
                onehot[at, :, i * 128:(i + 1) * 128] = hit

        def columns(i, carry):
            @pl.when(c == 0)
            def _():
                table_copy(i).wait()

            found = jnp.dot(onehot[...].reshape(toks, vocab_pad), tab[i], preferred_element_type=jnp.float32)
            at = pl.ds(pl.multiple_of(i * tab_tile, 128), tab_tile)
            part_ref[c, :, :, at] = found.astype(jnp.bfloat16).reshape(4, t4, tab_tile)
            return carry

        lax.fori_loop(0, n_tab, columns, 0)
        core_rs(c).start()

        @pl.when(c == 0)
        def _():
            for copy in w_copies:
                copy.start()

    def s1(c):
        core_rs(c).wait_recv()
        xsend[c] = part_ref[c, q_x] + crs[c, 1 - xx]
        x_rs(c).start()
        zown[c] = part_ref[c, q_own] + crs[c, xx]

    def s2(c):
        x_rs(c).wait_recv()
        zown[c] = zown[c] + xrs[c]

        @pl.when(jnp.logical_not(inner))
        def _():
            z_far_end(c).start()

    def s3(c):
        @pl.when(inner)
        def _():
            z_wait(near_slot, c)
            zfar_out[c] = zown[c] + zin[near_slot, c]
            z_far_inner(c).start()

    def s4(c):
        z_wait(far_slot, c)

        @pl.when(inner)
        def _():
            znear_out[c] = zown[c] + zin[far_slot, c]
            z_near(c).start()
            act[c, q_own] = zfar_out[c] + zin[far_slot, c]

        @pl.when(jnp.logical_not(inner))
        def _():
            act[c, q_own] = zown[c] + zin[far_slot, c]

        x_ag(c, q_own).start()
        core_ag(c, q_own, 0).start()

    def s5(c):
        x_ag(c, q_x).wait_recv()
        core_ag(c, q_x, 1).start()

    def s6(c):
        core_ag(c, q_c0, 0).wait_recv()
        core_ag(c, q_c1, 1).wait_recv()

        @pl.when(c == 0)
        def _():
            for copy in w_copies:
                copy.wait()

        gain = gain_ref[:, pl.ds(pl.multiple_of(col * dk, 128), dk)]
        values = act[c].reshape(toks, dk).astype(jnp.float32)
        squares = jnp.sum(values * values, axis=1, keepdims=True)
        xbuf[...] = (values * gain).astype(jnp.bfloat16)
        high = squares.astype(jnp.bfloat16)
        low = (squares - high.astype(jnp.float32)).astype(jnp.bfloat16)
        tail = width - qo - nq
        lane = lax.broadcasted_iota(jnp.int32, (toks, tail), 1)
        pf[c, :, :, qo + nq:] = jnp.broadcast_to(squares, (toks, tail)).reshape(n_col, rows, tail)
        both = jnp.where(lane == 0, high.astype(jnp.float32), low.astype(jnp.float32)).astype(jnp.bfloat16)
        ysend[c, :, :, qo + nq:] = both.reshape(n_col, rows, tail)

        def put(start, out, size):
            out = out.reshape(n_col, rows, size)
            pf[c, :, :, pl.ds(start, size)] = out
            ysend[c, :, :, pl.ds(start, size)] = out.astype(jnp.bfloat16)

        put(
            qo,
            lax.dot_general(xbuf[...], wq[...], (((1,), (1,)), ((), ())), preferred_element_type=jnp.float32), nq,
        )
        for d in range(1, n_col):
            y_send(c, d, pieces).start()

        def tiles(j, carry):
            at = pl.ds(pl.multiple_of(j * TILE, TILE), TILE)
            start = pl.multiple_of(2 * j * TILE, TILE)
            put(start, jnp.dot(xbuf[...], wg[:, at], preferred_element_type=jnp.float32), TILE)
            put(
                pl.multiple_of(start + TILE, TILE),
                jnp.dot(xbuf[...], wu[:, at], preferred_element_type=jnp.float32), TILE,
            )
            for d in range(1, n_col):
                y_send(c, d, j).start()
            return carry

        lax.fori_loop(0, pieces, tiles, 0)

    def s7(c):
        peers = [(col + d) % n_col for d in range(1, n_col)]

        def total(start, size):
            at = pl.ds(start, size)
            value = pf[c, col, :, at]
            for peer in peers:
                value = value + yrecv[c, peer, :, at].astype(jnp.float32)
            return value

        y_wait(c, pieces)
        squares = pf[c, col, :, qo + nq:qo + nq + 1]
        for peer in peers:
            squares = squares + yrecv[c, peer, :, qo + nq:qo + nq + 1].astype(jnp.float32)
            squares = squares + yrecv[c, peer, :, qo + nq + 1:qo + nq + 2].astype(jnp.float32)
        factor = lax.rsqrt(squares / features + eps)
        q_ref[c] = (total(qo, nq) * factor).astype(jnp.bfloat16)

        def tiles(j, carry):
            y_wait(c, j)
            start = pl.multiple_of(2 * j * TILE, TILE)
            gate = total(start, TILE) * factor
            up = total(pl.multiple_of(start + TILE, TILE), TILE) * factor
            at = pl.ds(pl.multiple_of(j * TILE, TILE), TILE)
            h_ref[c, :, at] = (gate / (1.0 + jnp.exp(-gate)) * up).astype(jnp.bfloat16)
            return carry

        lax.fori_loop(0, pieces, tiles, 0)

    stages = ((1, s1), (2, s2), (3, s3), (4, s4), (5, s5), (0, s0), (6, s6), (7, s7))

    def tick(t, carry):
        for s, run in stages:
            at_stage(t, s, run)
        return carry

    lax.fori_loop(0, chunks + len(stages) - 1, tick, 0)

    def finish(c, carry):
        core_rs(c).wait_send()
        x_rs(c).wait_send()
        z_far_end(c).wait_send()

        @pl.when(inner)
        def _():
            z_near(c).wait_send()

        x_ag(c, q_own).wait_send()
        core_ag(c, q_own, 0).wait_send()
        core_ag(c, q_x, 1).wait_send()
        for d in range(1, n_col):
            for j in range(pieces + 1):
                y_send(c, d, j).wait_send()
        return carry

    lax.fori_loop(0, chunks, finish, 0)
    for d in range(1, n_col):
        id_send(d).wait_send()


def body(n_row, n_col, token_ids, table, norm_gain, w_qkv, w_gate, w_up):
    chunks = CHUNKS
    vocab_rows, dk = table.shape
    mine = token_ids.shape[0]
    rows = mine // chunks
    t4 = n_col * rows // 4
    nq, nf = w_qkv.shape[1], w_gate.shape[1]
    width = 2 * nf + (nq + 2 + 127) // 128 * 128
    ids = token_ids.reshape(chunks, 1, rows)
    tab_tile = 512 if dk % 512 == 0 else 128
    n_tab = dk // tab_tile
    vocab_pad = (vocab_rows + 127) // 128 * 128
    pieces = nf // TILE
    bf = jnp.bfloat16
    dma = pltpu.SemaphoreType.DMA
    vmem = pl.BlockSpec(memory_space=pltpu.VMEM)
    hbm = pl.BlockSpec(memory_space=pl.ANY)
    q, h = pl.pallas_call(
        functools.partial(kernel, n_row, n_col, chunks, width, dk * n_col),
        out_shape=(
            jax.ShapeDtypeStruct((chunks, rows, nq), bf),
            jax.ShapeDtypeStruct((chunks, rows, nf), bf),
        ),
        in_specs=[vmem, hbm, vmem, hbm, hbm, hbm],
        out_specs=(vmem, vmem),
        scratch_shapes=[
            pltpu.VMEM((n_tab, vocab_pad, tab_tile), bf),
            pltpu.VMEM((n_col, chunks, 1, rows), jnp.int32),
            pltpu.VMEM((n_col, rows, vocab_pad), bf),
            pltpu.VMEM((chunks, 4, t4, dk), bf),
            pltpu.VMEM((nq, dk), bf),
            pltpu.VMEM(w_gate.shape, bf),
            pltpu.VMEM(w_up.shape, bf),
            pltpu.VMEM((chunks, 2, t4, dk), bf),
            pltpu.VMEM((chunks, t4, dk), bf),
            pltpu.VMEM((chunks, t4, dk), bf),
            pltpu.VMEM((chunks, t4, dk), bf),
            pltpu.VMEM((2, chunks, t4, dk), bf),
            pltpu.VMEM((chunks, t4, dk), bf),
            pltpu.VMEM((chunks, t4, dk), bf),
            pltpu.VMEM((chunks, 4, t4, dk), bf),
            pltpu.VMEM((4 * t4, dk), bf),
            pltpu.VMEM((chunks, n_col, rows, width), jnp.float32),
            pltpu.VMEM((chunks, n_col, rows, width), bf),
            pltpu.VMEM((chunks, n_col, rows, width), bf),
            dma((n_tab,)), dma((max(n_col - 1, 1),)), dma((n_col,)),
            dma((3,)),
            dma((chunks,)), dma((chunks,)),
            dma((chunks,)), dma((chunks,)),
            dma((chunks,)), dma((chunks,)), dma((2, chunks)),
            dma((chunks,)), dma((chunks,)),
            dma((chunks, 2)), dma((chunks, 2)),
            dma((chunks, max(n_col - 1, 1), pieces + 1)), dma((chunks, n_col, pieces + 1)),
        ],
        compiler_params=pltpu.CompilerParams(
            collective_id=0, has_side_effects=True, vmem_limit_bytes=62 * 1024 * 1024
        ),
    )(ids, table, norm_gain.reshape(1, -1), w_qkv.T, w_gate, w_up)
    return q.reshape(mine, nq), h.reshape(mine, nf)


def solution(mesh):
    return jax.shard_map(
        functools.partial(body, mesh.shape["row"], mesh.shape["col"]),
        mesh=mesh,
        in_specs=(
            P("col"),
            P("row", "col"),
            P(),
            P("col", "row"),
            P("col", "row"),
            P("col", "row"),
        ),
        out_specs=(P("col", "row"), P("col", "row")),
        check_vma=False,
    )
```
